32 devices in a mesh: lat: 4 (over z), lon: 8 (over y, x, core).
Axes of the slice: x: 2, y: 2, z: 4, core: 2. Of those that a mesh axis runs over, the one named last changes fastest.
Arguments:
- tokens: bfloat16 [48, 192, 512], P('lat', 'lon'), may hold values from -100 to 100
- fine_gain: float32 [512], replicated, may hold values from 0.5 to 1.5
- fine_qkv: bfloat16 [512, 768], replicated, may hold values from -20 to 20
- fine_proj: bfloat16 [256, 512], replicated, may hold values from -0.375 to 0.375
- merge_gain: float32 [2048], replicated, may hold values from 0.5 to 1.5
- merge_weight: bfloat16 [2048, 512], replicated, may hold values from -0.125 to 0.125
- coarse_gain: float32 [512], replicated, may hold values from 0.5 to 1.5
- coarse_qkv: bfloat16 [512, 1536], replicated, may hold values from -20 to 20
- coarse_proj: bfloat16 [512, 512], replicated, may hold values from -0.25 to 0.25
- cotangent: bfloat16 [24, 96, 512], P('lat', 'lon'), may hold values from -6 to 6
Outputs:
- output: bfloat16 [24, 96, 512], P('lat', 'lon')
- grad_tokens: bfloat16 [48, 192, 512], P('lat', 'lon')
- grad_fine_gain: float32 [512], P(('lat', 'lon'))
- grad_fine_qkv: float32 [512, 768], P(('lat', 'lon'))
- grad_fine_proj: float32 [256, 512], P(('lat', 'lon'))
- grad_merge_gain: float32 [2048], P(('lat', 'lon'))
- grad_merge_weight: float32 [2048, 512], P(('lat', 'lon'))
- grad_coarse_gain: float32 [512], P(('lat', 'lon'))
- grad_coarse_qkv: float32 [512, 1536], P(('lat', 'lon'))
- grad_coarse_proj: float32 [512, 512], P(('lat', 'lon'))
The draws below stay inside these ranges and needn't reach their ends.
All inputs are finite; a program needn't handle non-finite values.
Results may differ from the reference program's by a relative error of at most 0.028.
Values may be sent and summed in bfloat16 or wider, within the bound.
A program may use at most 128 MiB of HBM per device.

```python
import math
import jax
import jax.numpy as jnp
from jax import lax

D = 512
DC = 512
HD = 64
HF = 4
HC = 8
WLAT = 6
WLON = 12
SLAT = 3
SLON = 6
NLAT = 48
NLON = 192


def projection_draw(key, breadth, head_count):
    inner = head_count * HD
    keys_all = jax.random.split(key, 1)
    matrix = jnp.clip(jax.random.normal(keys_all[0], (breadth, 3 * inner), jnp.float32), -6.0, 6.0) * breadth ** (-0.5)
    return jnp.clip(matrix, -20.0, 20.0).astype(jnp.bfloat16)


def draw_tokens(key, part):
    keys_all = jax.random.split(jax.random.fold_in(key, 11), 3)
    row_scale = jnp.exp(jax.random.uniform(keys_all[0], (NLAT, NLON, 1), jnp.float32, 0.0, math.log(10.0)))
    channel_scale = jnp.exp(jax.random.uniform(keys_all[1], (1, 1, D), jnp.float32, -0.7, 0.7))
    base_values = jax.random.normal(keys_all[2], (NLAT, NLON, D), jnp.float32)
    return jnp.clip(base_values * row_scale * channel_scale, -100.0, 100.0).astype(jnp.bfloat16)


def draw_fine_qkv(key, part):
    return projection_draw(jax.random.fold_in(key, 23), D, HF)


def draw_coarse_qkv(key, part):
    return projection_draw(jax.random.fold_in(key, 37), DC, HC)


def level_of(stream_key, extent, shards, least, high):
    factor_of = 1.0
    for position, blocks in shards:
        heights = jax.random.uniform(jax.random.fold_in(jax.random.fold_in(stream_key, 6), position), (blocks,), jnp.float32, least / len(shards), high / len(shards))
        factor_of = factor_of * jnp.repeat(jnp.exp(heights), extent[position] // blocks).reshape((-1,) + (1,) * (len(extent) - 1 - position))
    return factor_of


def centred(own_key, shape, scale, bound, pieces=(), kind=jnp.bfloat16):
    gain = level_of(own_key, shape, pieces, -0.22, 0.18) if pieces else 1.0
    values = jax.random.normal(own_key, shape, jnp.float32) * scale * gain
    return jnp.minimum(jnp.maximum(values, -bound), bound).astype(kind)


def setup_inputs(seed: int = 0) -> dict:
    streams_of = jax.random.split(jax.random.key(seed), 11)
    tokens = draw_tokens(jax.random.fold_in(streams_of[10], 71), 0)
    fine_gain = jnp.clip(1.0 + 0.1 * jax.random.normal(streams_of[1], (D,), jnp.float32), 0.5, 1.5)
    fine_qkv = draw_fine_qkv(jax.random.fold_in(streams_of[10], 71), 0)
    fine_proj = centred(streams_of[3], (HF * HD, D), (HF * HD) ** -0.5, 0.375)
    merge_gain = jnp.clip(1.0 + 0.1 * jax.random.normal(streams_of[4], (4 * D,), jnp.float32), 0.5, 1.5)
    merge_weight = centred(streams_of[5], (4 * D, DC), (4 * D) ** -0.5, 0.125)
    coarse_gain = jnp.clip(1.0 + 0.1 * jax.random.normal(streams_of[6], (DC,), jnp.float32), 0.5, 1.5)
    coarse_qkv = draw_coarse_qkv(jax.random.fold_in(streams_of[10], 71), 0)
    coarse_proj = centred(streams_of[8], (HC * HD, DC), (HC * HD) ** -0.5, 0.25)
    cotangent = centred(streams_of[9], (NLAT // 2, NLON // 2, DC), 1.0, 6.0, ((0, 4), (1, 8)))
    return {"tokens": tokens, "fine_gain": fine_gain, "fine_qkv": fine_qkv, "fine_proj": fine_proj, "merge_gain": merge_gain, "merge_weight": merge_weight, "coarse_gain": coarse_gain, "coarse_qkv": coarse_qkv, "coarse_proj": coarse_proj, "cotangent": cotangent}


EPSILON = 1e-05

def layer_norm(values, gains):
    center = lax.optimization_barrier(jnp.mean(values, axis=-1, keepdims=True))
    shifted = values - center
    spread = lax.optimization_barrier(jnp.mean(shifted * shifted, axis=-1, keepdims=True))
    return shifted * lax.rsqrt(spread + EPSILON) * gains

def window_attention(packed, row_offset, total_rows, head_count):
    row_count, col_count = (packed.shape[0], packed.shape[1])
    head_size = packed.shape[2] // (3 * head_count)
    lat_windows = row_count // WLAT
    lon_windows = col_count // WLON
    grouped = packed.reshape(lat_windows, WLAT, lon_windows, WLON, 3, head_count, head_size)
    grouped = grouped.transpose(4, 0, 2, 5, 1, 3, 6).reshape(3, lat_windows, lon_windows, head_count, WLAT * WLON, head_size)
    queries = grouped[0].astype(jnp.float32)
    keys_all = grouped[1].astype(jnp.float32)
    values_all = grouped[2].astype(jnp.float32)
    scores = jnp.einsum('abhqd,abhkd->abhqk', queries, keys_all) * head_size ** (-0.5)
    row_index = row_offset + jnp.arange(row_count, dtype=jnp.int32)
    region = (row_index >= total_rows - SLAT).reshape(lat_windows, WLAT)
    region = jnp.broadcast_to(region[:, :, None], (lat_windows, WLAT, WLON)).reshape(lat_windows, WLAT * WLON)
    allowed = region[:, None, None, :, None] == region[:, None, None, None, :]
    scores = jnp.where(allowed, scores, -1000000000.0)
    largest = lax.optimization_barrier(jnp.max(scores, axis=-1, keepdims=True))
    exponent = jnp.exp(scores - largest)
    attn_weights = (exponent / lax.optimization_barrier(jnp.sum(exponent, axis=-1, keepdims=True))).astype(jnp.bfloat16)
    mixed_out = jnp.einsum('abhqk,abhkd->abhqd', attn_weights.astype(jnp.float32), values_all).astype(jnp.bfloat16)
    mixed_out = mixed_out.reshape(lat_windows, lon_windows, head_count, WLAT, WLON, head_size)
    return mixed_out.transpose(0, 3, 1, 4, 2, 5).reshape(row_count, col_count, head_count * head_size)

def block_forward(rolled, gains, weight_qkv, weight_proj, row_offset, total_rows, head_count):
    normed = layer_norm(rolled.astype(jnp.float32), gains).astype(jnp.bfloat16)
    packed = jnp.dot(normed, weight_qkv, preferred_element_type=jnp.float32).astype(jnp.bfloat16)
    mixed_out = window_attention(packed, row_offset, total_rows, head_count)
    added = jnp.dot(mixed_out, weight_proj, preferred_element_type=jnp.float32)
    result = (rolled.astype(jnp.float32) + added).astype(jnp.bfloat16)
    return (result, (normed, packed, mixed_out))

def block_backward(grad_out, rolled, gains, weight_qkv, weight_proj, saved, row_offset, total_rows, head_count):
    normed, packed, mixed_out = saved
    grad_mixed = lax.dot_general(grad_out, weight_proj, (((2,), (1,)), ((), ())), preferred_element_type=jnp.float32).astype(jnp.bfloat16)
    grad_proj = lax.dot_general(mixed_out, grad_out, (((0, 1), (0, 1)), ((), ())), preferred_element_type=jnp.float32)

    def attend_only(packed_in):
        return window_attention(packed_in, row_offset, total_rows, head_count)
    _, attend_back = jax.vjp(attend_only, packed)
    grad_packed = attend_back(grad_mixed)[0]
    grad_normed = lax.dot_general(grad_packed, weight_qkv, (((2,), (1,)), ((), ())), preferred_element_type=jnp.float32).astype(jnp.bfloat16)
    grad_qkv = lax.dot_general(normed, grad_packed, (((0, 1), (0, 1)), ((), ())), preferred_element_type=jnp.float32)
    _, norm_back = jax.vjp(layer_norm, rolled.astype(jnp.float32), gains)
    grad_input, grad_gain = norm_back(grad_normed.astype(jnp.float32))
    grad_rolled = (grad_out.astype(jnp.float32) + grad_input).astype(jnp.bfloat16)
    return (grad_rolled, grad_gain, grad_qkv, grad_proj)

def merge_tokens(patch_grid):
    row_count, col_count, breadth = patch_grid.shape
    reshaped = patch_grid.reshape(row_count // 2, 2, col_count // 2, 2, breadth)
    return reshaped.transpose(0, 2, 3, 1, 4).reshape(row_count // 2, col_count // 2, 4 * breadth)

def split_tokens(merged_grid):
    row_count, col_count, breadth = merged_grid.shape
    narrow = breadth // 4
    reshaped = merged_grid.reshape(row_count, col_count, 2, 2, narrow)
    return reshaped.transpose(0, 3, 1, 2, 4).reshape(2 * row_count, 2 * col_count, narrow)

def merge_forward(fine_grid, gains, weight):
    packed_grid = merge_tokens(fine_grid)
    normed = layer_norm(packed_grid.astype(jnp.float32), gains).astype(jnp.bfloat16)
    merged = jnp.dot(normed, weight, preferred_element_type=jnp.float32).astype(jnp.bfloat16)
    return (merged, (packed_grid, normed))

def merge_backward(grad_merged, saved, gains, weight):
    packed_grid, normed = saved
    grad_normed = lax.dot_general(grad_merged, weight, (((2,), (1,)), ((), ())), preferred_element_type=jnp.float32).astype(jnp.bfloat16)
    grad_weight = lax.dot_general(normed, grad_merged, (((0, 1), (0, 1)), ((), ())), preferred_element_type=jnp.float32)
    _, norm_back = jax.vjp(layer_norm, packed_grid.astype(jnp.float32), gains)
    grad_packed, grad_gain = norm_back(grad_normed.astype(jnp.float32))
    return (split_tokens(grad_packed.astype(jnp.bfloat16)), grad_gain, grad_weight)

def reference(tokens, fine_gain, fine_qkv, fine_proj, merge_gain, merge_weight, coarse_gain, coarse_qkv, coarse_proj, cotangent):
    fine_total = tokens.shape[0]
    coarse_total = fine_total // 2
    grad_scale = (tokens.shape[0] * tokens.shape[1] // 4) ** (-0.5)
    start = jnp.int32(0)
    rolled_fine = jnp.roll(tokens, (-SLAT, -SLON), axis=(0, 1))
    fine_result, fine_saved = block_forward(rolled_fine, fine_gain, fine_qkv, fine_proj, start, fine_total, HF)
    fine_grid = jnp.roll(fine_result, (SLAT, SLON), axis=(0, 1))
    merged, merge_saved = merge_forward(fine_grid, merge_gain, merge_weight)
    rolled_coarse = jnp.roll(merged, (-SLAT, -SLON), axis=(0, 1))
    coarse_result, coarse_saved = block_forward(rolled_coarse, coarse_gain, coarse_qkv, coarse_proj, start, coarse_total, HC)
    output = jnp.roll(coarse_result, (SLAT, SLON), axis=(0, 1))
    grad_coarse_out = jnp.roll(cotangent, (-SLAT, -SLON), axis=(0, 1))
    grad_rolled_coarse, coarse_gain_sum, coarse_qkv_sum, coarse_proj_sum = block_backward(grad_coarse_out, rolled_coarse, coarse_gain, coarse_qkv, coarse_proj, coarse_saved, start, coarse_total, HC)
    grad_merged = jnp.roll(grad_rolled_coarse, (SLAT, SLON), axis=(0, 1))
    grad_fine_grid, merge_gain_sum, merge_weight_sum = merge_backward(grad_merged, merge_saved, merge_gain, merge_weight)
    grad_fine_out = jnp.roll(grad_fine_grid, (-SLAT, -SLON), axis=(0, 1))
    grad_rolled_fine, fine_gain_sum, fine_qkv_sum, fine_proj_sum = block_backward(grad_fine_out, rolled_fine, fine_gain, fine_qkv, fine_proj, fine_saved, start, fine_total, HF)
    grad_tokens = jnp.roll(grad_rolled_fine, (SLAT, SLON), axis=(0, 1))
    return (output, grad_tokens, fine_gain_sum * grad_scale, fine_qkv_sum * grad_scale, fine_proj_sum * grad_scale, merge_gain_sum * grad_scale, merge_weight_sum * grad_scale, coarse_gain_sum * grad_scale, coarse_qkv_sum * grad_scale, coarse_proj_sum * grad_scale)
```

```python
import functools
import itertools
import types

import jax
import jax.numpy as jnp
import numpy as np
from jax import lax
from jax.experimental import pallas as pl
from jax.experimental.pallas import tpu as pltpu
from jax.sharding import PartitionSpec as P

HF = 4
HC = 8
WLAT = 6
WLON = 12
SLAT = 3
SLON = 6


EPSILON = 1e-05


VMEM = pl.BlockSpec(memory_space=pltpu.VMEM)
ANY = pl.BlockSpec(memory_space=pl.ANY)
LAT, LON = "lat", "lon"
F32 = jnp.float32
BF16 = jnp.bfloat16


def one_hot(sources, size):
    matrix = np.zeros((len(sources), size), np.float32)
    for row, source in enumerate(sources):
        if source >= 0:
            matrix[row, source] = 1.0
    return matrix


def window_order(rows, cols):
    return [
        (a * WLAT + i, b * WLON + j)
        for a in range(rows // WLAT)
        for b in range(cols // WLON)
        for i in range(WLAT)
        for j in range(WLON)
    ]


def merge_order(rows, cols):
    return [
        (2 * a + low, 2 * b + side)
        for side in range(2)
        for low in range(2)
        for a, b in window_order(rows // 2, cols // 2)
    ]


def natural_order(rows, cols):
    return [(i, j) for i in range(rows) for j in range(cols)]


def roll_parts(rows, cols, ahead):
    if ahead:
        lat, lon = (range(SLAT), range(SLAT, rows)), (range(SLON), range(SLON, cols))
    else:
        lat = (range(rows - SLAT, rows), range(rows - SLAT))
        lon = (range(cols - SLON, cols), range(cols - SLON))
    pick = ((lat[0], lon[1]), (lat[1], lon[0]), (lat[0], lon[0]))
    return [[(i, j) for i in r for j in c] for r, c in pick]


def roll_matrices(rows, cols, ahead, order):
    shift = 1 if ahead else -1
    parts = [{cell: k for k, cell in enumerate(p)} for p in roll_parts(rows, cols, ahead)]
    found = [[], [], [], []]
    for i, j in order:
        row, col = i + shift * SLAT, j + shift * SLON
        out_row, out_col = not 0 <= row < rows, not 0 <= col < cols
        cell = (row % rows, col % cols)
        which = {(0, 0): 0, (1, 0): 1, (0, 1): 2, (1, 1): 3}[(int(out_row), int(out_col))]
        for k in range(4):
            found[k].append((cell if k == 0 else parts[k - 1][cell]) if k == which else -1)
    return found, [len(p) for p in parts]


def assembling(rows, cols, ahead, order, stored):
    place = {cell: k for k, cell in enumerate(stored)}
    found, sizes = roll_matrices(rows, cols, ahead, order)
    own = [place[c] if c != -1 else -1 for c in found[0]]
    return [one_hot(own, rows * cols)] + [one_hot(f, n) for f, n in zip(found[1:], sizes)]


def sending(rows, cols, ahead, stored):
    place = {cell: k for k, cell in enumerate(stored)}
    return [
        one_hot([place[c] for c in part], rows * cols) for part in roll_parts(rows, cols, ahead)
    ]


def mm(left, right):
    return jnp.dot(left, right, preferred_element_type=F32)


def mm_t(left, right):
    return lax.dot_general(left, right, (((1,), (1,)), ((), ())), preferred_element_type=F32)


def t_mm(left, right):
    return lax.dot_general(left, right, (((0,), (0,)), ((), ())), preferred_element_type=F32)


def norm_parts(values):
    center = jnp.mean(values, axis=-1, keepdims=True)
    shifted = values - center
    spread = jnp.mean(shifted * shifted, axis=-1, keepdims=True)
    rate = lax.rsqrt(spread + EPSILON)
    return shifted * rate, rate


def norm_back(grad, unit, rate, gains):
    scaled = grad * gains
    first = jnp.mean(scaled, axis=-1, keepdims=True)
    second = jnp.mean(scaled * unit, axis=-1, keepdims=True)
    return rate * (scaled - first - unit * second), jnp.sum(grad * unit, axis=0, keepdims=True)


def lane_halves(value, size):
    lane = lax.broadcasted_iota(jnp.int32, value.shape, 1)
    return [
        jnp.where((lane >= k * size) & (lane < (k + 1) * size), value, jnp.zeros_like(value))
        for k in range(value.shape[1] // size)
    ]


def stacked(value, size):
    return jnp.concatenate(lane_halves(value, size), axis=0).astype(BF16)


def unstacked(value, size):
    cells = value.shape[0] * size // value.shape[1]
    lane = lax.broadcasted_iota(jnp.int32, (cells, value.shape[1]), 1)
    total = value[:cells]
    for k in range(1, value.shape[1] // size):
        total = jnp.where(lane >= k * size, value[k * cells : (k + 1) * cells], total)
    return total


def weights_of(query, keys, border, size):
    cells = keys.shape[0]
    scores = mm_t(query, keys) * size ** (-0.5)
    row = lax.broadcasted_iota(jnp.int32, scores.shape, 0)
    other = lax.broadcasted_iota(jnp.int32, scores.shape, 1)
    for _ in range(query.shape[0] // cells - 1):
        row = jnp.where(row >= cells, row - cells, row)
    allowed = (row >= border).astype(jnp.int32) == (other >= border).astype(jnp.int32)
    scores = jnp.where(allowed, scores, -1000000000.0)
    exponent = jnp.exp(scores - jnp.max(scores, axis=-1, keepdims=True))
    return exponent * (1.0 / jnp.sum(exponent, axis=-1, keepdims=True)), allowed


def attention_groups(cells, heads, inner, windows_lon):
    size = inner // heads
    lanes = 128 if inner % 128 == 0 and 128 % size == 0 else inner
    count = WLAT * WLON
    for window in range(cells // count):
        for start in range(0, inner, lanes):
            rows = slice(window * count, (window + 1) * count)
            yield window // windows_lon, rows, start, lanes, size


def border_of(edge, window_row):
    return (edge - window_row * WLAT) * WLON


def rounded(value):
    return value.astype(BF16).astype(F32)


def attend(packed, mixed_ref, saved, edge, heads, windows_lon):
    inner = packed.shape[1] // 3
    for k, (w, rows, start, lanes, size) in enumerate(
        attention_groups(packed.shape[0], heads, inner, windows_lon)
    ):
        query = stacked(packed[rows, start : start + lanes], size)
        keys = packed[rows, inner + start : inner + start + lanes].astype(BF16)
        vals = packed[rows, 2 * inner + start : 2 * inner + start + lanes].astype(BF16)
        weights, _ = weights_of(query, keys, border_of(edge, w), size)
        saved[k] = weights
        mixed_ref[rows, start : start + lanes] = unstacked(mm(weights.astype(BF16), vals), size)


def attend_back(packed, grad_mixed, grad_ref, saved, edge, heads, windows_lon, between=None):
    inner = packed.shape[1] // 3
    for k, (w, rows, start, lanes, size) in enumerate(
        attention_groups(packed.shape[0], heads, inner, windows_lon)
    ):
        query = stacked(packed[rows, start : start + lanes], size)
        keys = packed[rows, inner + start : inner + start + lanes].astype(BF16)
        vals = packed[rows, 2 * inner + start : 2 * inner + start + lanes].astype(BF16)
        grad = stacked(grad_mixed[rows, start : start + lanes], size)
        weights = saved[k]
        allowed = allowed_of(weights.shape, WLAT * WLON, border_of(edge, w))
        grad_weights = mm_t(grad, vals).astype(BF16).astype(F32)
        grad_vals = t_mm(weights.astype(BF16), grad)
        along = jnp.sum(grad_weights * weights, axis=-1, keepdims=True)
        slope = jnp.where(allowed, weights * (grad_weights - along), 0.0) * size ** (-0.5)
        slope = slope.astype(BF16)
        grad_ref[rows, start : start + lanes] = unstacked(mm(slope, keys), size)
        grad_ref[rows, inner + start : inner + start + lanes] = t_mm(slope, query)
        grad_ref[rows, 2 * inner + start : 2 * inner + start + lanes] = grad_vals
        if between is not None:
            between(k)


def allowed_of(shape, cells, border):
    row = lax.broadcasted_iota(jnp.int32, shape, 0)
    other = lax.broadcasted_iota(jnp.int32, shape, 1)
    for _ in range(shape[0] // cells - 1):
        row = jnp.where(row >= cells, row - cells, row)
    return (row >= border).astype(jnp.int32) == (other >= border).astype(jnp.int32)


def up16(count):
    return -(-count // 16) * 16


def part_sizes(rows, cols, ahead):
    return [up16(len(part)) for part in roll_parts(rows, cols, ahead)]


def assembler(rows, cols, ahead, order, stored):
    pieces = []
    for matrix in assembling(rows, cols, ahead, order, stored):
        width = matrix.shape[1]
        pieces.append(np.pad(np.asarray(matrix, np.float32), ((0, 0), (0, up16(width) - width))))
    return np.concatenate(pieces, axis=1)


def picker(rows, cols, ahead, stored):
    pieces = []
    for matrix in sending(rows, cols, ahead, stored):
        height = matrix.shape[0]
        pieces.append(np.pad(np.asarray(matrix, np.float32), ((0, up16(height) - height), (0, 0))))
    return np.concatenate(pieces, axis=0)


def padded(value):
    extra = up16(value.shape[0]) - value.shape[0]
    if extra:
        value = jnp.concatenate([value, jnp.zeros((extra, value.shape[1]), value.dtype)], axis=0)
    return value


def parity_matrix(run, parity):
    shape = (256, 256)
    source = lax.broadcasted_iota(jnp.int32, shape, 0)
    target = lax.broadcasted_iota(jnp.int32, shape, 1)
    side = (target // 128 + parity) % 2
    wanted = ((target % 128) // run * 2 + side) * run + target % run
    return (source == wanted).astype(F32).astype(BF16)


def by_parity(value, matrix):
    parts = [mm(value[:, b : b + 256], matrix) for b in range(0, value.shape[1], 256)]
    mine = jnp.concatenate([part[:, :128] for part in parts], axis=1).astype(BF16)
    other = jnp.concatenate([part[:, 128:] for part in parts], axis=1).astype(BF16)
    return mine, other


def joined(ref):
    value = ref[...]
    return value.reshape(value.shape[0] * value.shape[1], value.shape[2])


class Links:
    def __init__(self, lats, lons, sends, recvs):
        self.lats, self.lons, self.sends, self.recvs = lats, lons, sends, recvs
        self.lat, self.lon = lax.axis_index(LAT), lax.axis_index(LON)
        self.side, self.chip, self.chips = self.lon % 2, self.lon // 2, lons // 2
        self.ids, self.started = itertools.count(), []

    def at(self, lat_step, lon_step):
        lat = (self.lat + lat_step + self.lats) % self.lats
        return (lat, (self.lon + lon_step + self.lons) % self.lons)

    def partner(self):
        return (self.lat, self.lon + 1 - 2 * self.side)

    def chip_of(self, ahead):
        return (self.chip + ahead) % self.chips

    def same_side(self, ahead):
        return (self.lat, 2 * self.chip_of(ahead) + self.side)

    def send(self, source, target, device):
        index = next(self.ids)
        copy = pltpu.make_async_remote_copy(
            src_ref=source,
            dst_ref=target,
            send_sem=self.sends.at[index],
            recv_sem=self.recvs.at[index],
            device_id=device,
            device_id_type=pl.DeviceIdType.MESH,
        )
        copy.start()
        self.started.append(copy)
        return copy

    def greet(self):
        peers = [self.at(a, b) for s in (-1, 1) for a, b in ((s, 0), (0, s), (s, s))]
        peers += [self.at(0, step) for step in range(1, self.lons)]
        peers += [self.at(step, 0) for step in range(1, self.lats)]
        barrier = pltpu.get_barrier_semaphore()
        for peer in peers:
            pl.semaphore_signal(
                barrier, inc=1, device_id=peer, device_id_type=pl.DeviceIdType.MESH
            )
        return lambda: pl.semaphore_wait(barrier, len(peers))

    def exchange(self, out, target, own, sizes, ahead):
        s = -1 if ahead else 1
        copies, begin = [], 0
        for size, (a, b) in zip(sizes, ((s, 0), (0, s), (s, s))):
            there = target.at[pl.ds(own + begin, size)]
            copies.append(self.send(out.at[pl.ds(begin, size)], there, self.at(a, b)))
            begin += size
        return copies

    def near(self, level):
        step = 1 << level
        bit = (self.chip // step) % 2
        rest = self.chip // (2 * step) * step + self.chip % step
        count = self.chips // 2

        def at_rest(ahead):
            place = (rest + ahead) % count
            chip = place // step * (2 * step) + bit * step + place % step
            return (self.lat, 2 * chip + self.side)

        chip = self.chip + step - 2 * step * bit
        found = types.SimpleNamespace(bit=bit, quarter=2 * bit + self.side)
        found.same = (self.lat, 2 * chip + self.side)
        found.other = (self.lat, 2 * chip + 1 - self.side)
        found.ring = types.SimpleNamespace(place=rest, count=count, device=at_rest)
        return found

    def plane(self):
        return types.SimpleNamespace(place=self.chip, count=self.chips, device=self.same_side)

    def spread(self, slots, near):
        return [
            self.send(slots.at[0, 0], slots.at[1, 0], self.partner()),
            self.send(slots.at[0, 0], slots.at[0, 1], near.same),
        ]

    def relay(self, slots, copies):
        arrive(copies[1:])
        return copies[:1] + [self.send(slots.at[0, 1], slots.at[1, 1], self.partner())]

    def deal(self, pieces, slots, near):
        slots[0, 0] = pieces[near.quarter]
        mine, flip = 2 * near.bit, 2 - 2 * near.bit
        return [
            self.send(pieces.at[flip + self.side], slots.at[0, 1], near.same),
            self.send(pieces.at[flip + 1 - self.side], slots.at[1, 1], near.other),
            self.send(pieces.at[mine + 1 - self.side], slots.at[1, 0], self.partner()),
        ]


def arrive(copies):
    for copy in copies:
        copy.wait_recv()


class Sums:
    def __init__(self, links, ring, bufs, out, scale):
        self.links, self.ring, self.bufs = links, ring, bufs
        self.out, self.scale = out, scale

    def begin(self):
        links, ring, bufs = self.links, self.ring, self.bufs
        self.copies = []
        for ahead in range(1, ring.count):
            source = bufs.first.at[(ring.place + ahead) % ring.count]
            self.copies.append(links.send(source, bufs.land.at[ahead - 1], ring.device(ahead)))

    def middle(self):
        links, ring, bufs = self.links, self.ring, self.bufs
        arrive(self.copies)
        for row in range(links.lats):
            total = bufs.first[ring.place, row].astype(F32)
            for ahead in range(1, ring.count):
                total = total + bufs.land[ahead - 1, row].astype(F32)
            bufs.mid[row] = total.astype(bufs.mid.dtype)
        self.across()

    def across(self):
        links, bufs = self.links, self.bufs
        self.copies = [
            links.send(
                bufs.mid.at[(links.lat + ahead) % links.lats],
                bufs.last.at[ahead - 1],
                links.at(ahead, 0),
            )
            for ahead in range(1, links.lats)
        ]

    def end(self):
        links, bufs = self.links, self.bufs
        arrive(self.copies)
        total = bufs.mid[links.lat].astype(F32)
        for ahead in range(1, links.lats):
            total = total + bufs.last[ahead - 1].astype(F32)
        self.total = total * self.scale
        if self.out is not None:
            self.out[...] = self.total


def flat(ref):
    value = ref[...]
    count = 1
    for size in value.shape[:-1]:
        count *= size
    return value.reshape(count, value.shape[-1])


def mega_kernel(plan, *refs):
    tree = jax.tree.unflatten(plan.tree, refs)
    ins, res, buf, sums, sems = [types.SimpleNamespace(**part) for part in tree]
    lats, lons, fine, coarse, runs = plan.lats, plan.lons, plan.fine, plan.coarse, plan.runs
    links = Links(lats, lons, sems.sends, sems.recvs)
    cells, few = fine[0] * fine[1], coarse[0] * coarse[1]
    few16 = up16(few)
    wide, fine_wide = coarse[1] // WLON, fine[1] // WLON
    chips = lons // 2
    greeted = links.greet()

    loads = {}
    for k, name in enumerate(plan.loads):
        loads[name] = pltpu.make_async_copy(getattr(ins, name), buf.loads[name], sems.loads.at[k])
        loads[name].start()

    def load(name):
        if name in loads:
            loads.pop(name).wait()
        return buf.loads[name][...]

    names = types.SimpleNamespace(**{name: name for name in plan.loads})
    sizes, back_sizes = part_sizes(*fine, True), part_sizes(*fine, False)
    small, small_back = part_sizes(*coarse, True), part_sizes(*coarse, False)
    cat1, cat2, cat3, cat4 = buf.cats
    out1, out2, out3, out4 = buf.outs
    cat_c, cat_o = buf.small_cats
    out_c, out_o = buf.small_outs

    own_tokens = load(names.tokens)
    cat1[0:cells] = own_tokens
    out1[...] = mm(load(names.pick1), own_tokens).astype(BF16)
    greeted()
    halo1 = links.exchange(out1, cat1, cells, sizes, True)
    grid = load(names.cotangent)
    for i in range(coarse[0]):
        buf.cot[i * coarse[1] : (i + 1) * coarse[1]] = grid[i].astype(F32)
    own_cot = padded(buf.cot[...]).astype(BF16)
    cat_c[0:few16] = own_cot
    out_c[...] = mm(load(names.pick_c), own_cot).astype(BF16)
    halo_c = links.exchange(out_c, cat_c, few16, small, True)
    edge = plan.fine_total - SLAT - links.lat * fine[0]
    coarse_edge = plan.coarse_total - SLAT - links.lat * coarse[0]
    split = {
        run: parity_matrix(run, links.side)
        for run in sorted({runs.fine_qkv, runs.fine_proj, runs.coarse_proj})
    }

    gather1 = load(names.gather1)
    arrive(halo1)
    x1 = mm(gather1, cat1[...])
    unit1, rate1 = norm_parts(x1)
    gains1 = load(names.fine_gain)
    normed1 = (unit1 * gains1).astype(BF16)
    buf.unit1[...] = unit1
    buf.rate1[...] = rate1
    w_qkv1 = load(names.fine_qkv)
    packed1 = rounded(mm(normed1, w_qkv1))
    buf.packed1[...] = packed1
    attend(packed1, buf.mixed1, buf.saved1, edge, HF, fine_wide)
    blend1 = buf.mixed1[...].astype(BF16)
    w_proj1 = load(names.fine_proj)
    y1 = (x1 + mm(blend1, w_proj1)).astype(BF16)
    cat2[0:cells] = y1
    out2[...] = mm(load(names.pick2), y1).astype(BF16)
    halo2 = links.exchange(out2, cat2, cells, sizes, True)

    def to_partner(pair):
        return links.send(pair.at[0], pair.at[1], links.partner())

    def halves(value, run, pair, out):
        mine, other = by_parity(value, split[run])
        pair[0] = mine
        out[...] = other
        return links.send(out, pair.at[1], links.partner())

    pair_fq = halves(normed1, runs.fine_qkv, buf.fq_l, buf.fq_o)
    pair_fp = halves(blend1, runs.fine_proj, buf.fp_l, buf.fp_o)
    gather_c = load(names.gather_c)
    arrive(halo_c)
    dy2 = mm(gather_c, cat_c[...])
    buf.cp_r[0] = padded(dy2).astype(BF16)
    pair_dy2 = to_partner(buf.cp_r)
    w_proj2 = load(names.coarse_proj)
    grad_mixed2 = rounded(mm_t(dy2.astype(BF16), w_proj2))
    gather2 = load(names.gather2)
    merge_gains, w_merge = load(names.merge_gain), load(names.merge_weight)
    gains2, w_qkv2 = load(names.coarse_gain), load(names.coarse_qkv)
    arrive(halo2)

    spread = mm(gather2, cat2[...])
    packed_grid = jnp.concatenate([spread[k * few : (k + 1) * few] for k in range(4)], axis=1)
    merge_unit, merge_rate = norm_parts(packed_grid)
    merge_scaled = padded(merge_unit * merge_gains)
    merge_normed = merge_scaled.astype(BF16)
    x2 = rounded(mm(merge_normed, w_merge)[:few])
    near_m, near_q = links.near(min(1, chips.bit_length() - 2)), links.near(0)
    run = runs.merge_weight
    level = min(1, chips.bit_length() - 2)
    for q in range(4):
        parts = []
        for r in range(chips // 2):
            chip = (r >> level << level + 1) + (q // 2 << level) + r % (1 << level)
            parts += [((k * chips + chip) * 2 + q % 2) * run for k in range(lats)]
        piece = jnp.concatenate([merge_scaled[:, p : p + run] for p in parts], axis=1)
        buf.m_pieces[q] = piece.astype(BF16)
    sent_m = links.deal(buf.m_pieces, buf.m_l, near_m)
    unit2, rate2 = norm_parts(x2)
    normed2 = padded(unit2 * gains2).astype(BF16)
    buf.q_l[0, 0] = normed2
    sent_n = links.spread(buf.q_l, near_q)
    packed2 = rounded(mm(normed2, w_qkv2)[:few])
    attend(packed2, buf.mixed2, buf.saved2, coarse_edge, HC, wide)
    blend2 = padded(buf.mixed2[...]).astype(BF16)
    pair_p = halves(blend2, runs.coarse_proj, buf.cp_l, buf.cp_o)

    attend_back(packed2, grad_mixed2, buf.grad2, buf.saved2, coarse_edge, HC, wide)
    grad2 = padded(buf.grad2[...])
    grad_packed2 = grad2.astype(BF16)
    share = grad2.shape[1] // 4
    for q in range(4):
        buf.q_pieces[q] = grad2[:, q * share : (q + 1) * share].astype(BF16)
    sent_q = links.deal(buf.q_pieces, buf.q_r, near_q)

    def reduced(left, right, run, total):
        value = t_mm(flat(left), flat(right))
        width = value.shape[1]
        for row in range(lats):
            for chip in range(chips):
                begin = (row * chips + chip) * run
                piece = value[begin : begin + run].astype(BF16)
                total.bufs.first[chip, row, :, 0:width] = piece
        return width

    place = lax.broadcasted_iota(jnp.int32, (lats * chips, 128), 0)
    lane = lax.broadcasted_iota(jnp.int32, (lats * chips, 128), 1)
    owner = (place % lats) * lons + (place // lats) * 2 + links.side
    fold_row = lax.broadcasted_iota(jnp.int32, (128, 128), 0)
    fold_col = lax.broadcasted_iota(jnp.int32, (128, 128), 1)

    def deal_gains(value, total, start):
        run = value.shape[1] // (lats * lons)
        picked = jnp.zeros((lats * chips, 128), F32)
        for b in range(0, value.shape[1], 128):
            row = jnp.broadcast_to(value[:, b : b + 128], (lats * chips, 128))
            picked = picked + jnp.where((lane + b) // run == owner, row, 0.0)
        fold = (fold_row % run == fold_col).astype(BF16)
        folded = mm(picked.astype(BF16), fold)
        target = total.bufs.first
        shape = (target.shape[2], 128)
        for p in range(lats * chips):
            rows = jnp.broadcast_to(folded[p : p + 1], shape).astype(BF16)
            target[p // lats, p % lats, :, start : start + 128] = rows

    grad_normed2 = rounded(mm_t(grad_packed2, w_qkv2)[:few])
    grad_in2, gain_sum2 = norm_back(grad_normed2, unit2, rate2, gains2)
    dz = padded(dy2 + grad_in2).astype(BF16)
    buf.m_r[0, 0] = dz
    grad_merge = rounded(mm_t(dz, w_merge)[:few])
    grad_grid, merge_sum = norm_back(grad_merge, merge_unit, merge_rate, merge_gains)
    breadth = spread.shape[1]
    df = jnp.concatenate(
        [grad_grid[:, k * breadth : (k + 1) * breadth] for k in range(4)], axis=0
    ).astype(BF16)
    cat3[0:cells] = df
    out3[...] = mm(load(names.pick3), df).astype(BF16)
    halo3 = links.exchange(out3, cat3, cells, back_sizes, False)
    sent_z = links.spread(buf.m_r, near_m)
    merge_count = merge_sum.shape[1]
    buf.gain2[0, :, 0:merge_count] = merge_sum
    buf.gain2[0, :, merge_count:] = gain_sum2
    pair_g2 = to_partner(buf.gain2)
    relay_n = links.relay(buf.q_l, sent_n)

    def sum_of(name, out, ring):
        bufs = types.SimpleNamespace(**getattr(sums, name))
        return Sums(links, ring, bufs, out, plan.scale)

    keys = types.SimpleNamespace(**{name: name for name in vars(sums)})
    total_p = sum_of(keys.coarse_proj, res.coarse_proj, links.plane())
    total_q = sum_of(keys.coarse_qkv, None, near_q.ring)
    total_m = sum_of(keys.merge_weight, res.merge_weight, near_m.ring)
    total_fp = sum_of(keys.fine_proj, res.fine_proj, links.plane())
    total_fq = sum_of(keys.fine_qkv, res.fine_qkv, links.plane())

    arrive([pair_p, pair_dy2])
    width_p = reduced(buf.cp_l, buf.cp_r, runs.coarse_proj, total_p)
    arrive([pair_g2])
    gains_both = buf.gain2[0] + buf.gain2[1]
    deal_gains(gains_both[:, :merge_count], total_p, width_p)
    deal_gains(gains_both[:, merge_count:], total_p, width_p + 128)
    total_p.begin()
    result2 = padded(x2 + mm(blend2, w_proj2)[:few]).astype(BF16)
    cat_o[0:few16] = result2
    out_o[...] = mm(load(names.pick_o), result2).astype(BF16)
    halo_o = links.exchange(out_o, cat_o, few16, small_back, False)
    gather3 = load(names.gather3)
    arrive(halo3)

    dy1 = mm(gather3, cat3[...])
    dy1_low = dy1.astype(BF16)
    buf.fp_r[0] = dy1_low
    pair_dy1 = to_partner(buf.fp_r)
    grad_mixed1 = rounded(mm_t(dy1_low, w_proj1))

    steps = types.SimpleNamespace()

    def reduce_near(left, right, total, by_row):
        value = t_mm(flat(left), flat(right))
        count = total.ring.count
        tall = value.shape[0] // (lats * count)
        for row in range(lats):
            for place in range(count):
                begin = (row * count + place if by_row else place * lats + row) * tall
                total.bufs.first[place, row] = value[begin : begin + tall].astype(BF16)
        total.begin()

    def between1(k):
        if k == 0:
            steps.relay_z = links.relay(buf.m_r, sent_z)
        if k == 1:
            arrive(sent_q + relay_n)
            reduce_near(buf.q_l, buf.q_r, total_q, True)
        if k == 2:
            arrive([pair_fp, pair_dy1])
            reduced(buf.fp_l, buf.fp_r, runs.fine_proj, total_fp)
            total_fp.begin()
        if k == 3:
            arrive(steps.relay_z + sent_m)
            reduce_near(buf.m_l, buf.m_r, total_m, False)
        if k == 5:
            total_p.middle()
        if k == 7:
            total_q.middle()

    attend_back(
        buf.packed1[...], grad_mixed1, buf.grad1, buf.saved1, edge, HF, fine_wide, between1
    )
    grad_packed1 = buf.grad1[...].astype(BF16)
    buf.fq_r[0] = grad_packed1
    pair_dp1 = to_partner(buf.fq_r)
    grad_normed1 = rounded(mm_t(grad_packed1, w_qkv1))
    grad_in1, gain_sum1 = norm_back(grad_normed1, buf.unit1[...], buf.rate1[...], gains1)
    buf.gain1[0] = gain_sum1
    pair_g1 = to_partner(buf.gain1)
    dx1 = (dy1 + grad_in1).astype(BF16)
    cat4[0:cells] = dx1
    out4[...] = mm(load(names.pick4), dx1).astype(BF16)
    halo4 = links.exchange(out4, cat4, cells, back_sizes, False)
    arrive([pair_fq, pair_dp1])
    width_q = reduced(buf.fq_l, buf.fq_r, runs.fine_qkv, total_fq)
    arrive([pair_g1])
    deal_gains(buf.gain1[0] + buf.gain1[1], total_fq, width_q)
    total_fq.begin()
    total_p.end()
    total_fp.middle()
    total_m.middle()
    total_q.end()
    for q in range(4):
        high = total_q.total.shape[0] // 4
        buf.q_back[q] = total_q.total[q * high : (q + 1) * high]
    buf.q_parts[near_q.quarter] = buf.q_back[near_q.quarter]
    target = buf.q_parts.at[near_q.quarter]
    mine, flip = 2 * near_q.bit, 2 - 2 * near_q.bit
    sent_back = [
        links.send(buf.q_back.at[flip + links.side], target, near_q.same),
        links.send(buf.q_back.at[flip + 1 - links.side], target, near_q.other),
        links.send(buf.q_back.at[mine + 1 - links.side], target, links.partner()),
    ]
    arrive(halo_o)
    res.output[...] = mm(load(names.gather_o), cat_o[...])
    gather4 = load(names.gather4)
    arrive(halo4)
    res.tokens[...] = mm(gather4, cat4[...]).astype(BF16)
    total_fq.middle()
    arrive(sent_back)
    for q in range(4):
        res.coarse_qkv[:, q * share : (q + 1) * share] = buf.q_parts[q]
    total_fp.end()
    total_m.end()
    total_fq.end()
    for copy in links.started:
        copy.wait_send()


def finish_kernel(coarse, runs, *refs):
    ins, outs = refs[:7], refs[7:]
    output, tokens, qkv1, proj1, merge, qkv2, proj2 = ins
    for i in range(coarse[0]):
        outs[0][i] = output[i * coarse[1] : (i + 1) * coarse[1]].astype(BF16)
    outs[1][...] = tokens[...]
    for k, value in ((3, qkv1), (4, proj1), (6, merge), (8, qkv2), (9, proj2)):
        outs[k][...] = value[:, : outs[k].shape[1]]
    wide1, wide2 = outs[3].shape[1], outs[9].shape[1]
    for k, value, begin in ((2, qkv1, wide1), (5, proj2, wide2), (7, proj2, wide2 + 128)):
        outs[k][...] = value[0:1, begin : begin + outs[k].shape[1]]


def local(
    tokens,
    fine_gain,
    fine_qkv,
    fine_proj,
    merge_gain,
    merge_weight,
    coarse_gain,
    coarse_qkv,
    coarse_proj,
    cotangent,
):
    lats, lons = lax.axis_size(LAT), lax.axis_size(LON)
    devices, chips = lats * lons, lons // 2
    fine = tokens.shape[:2]
    coarse = (fine[0] // 2, fine[1] // 2)
    cells, few = fine[0] * fine[1], coarse[0] * coarse[1]
    few16 = up16(few)
    breadth, inner, inner2 = tokens.shape[2], fine_proj.shape[0], coarse_proj.shape[0]
    depth = coarse_proj.shape[1]
    windowed, natural, merged = window_order(*fine), natural_order(*fine), merge_order(*fine)
    coarse_windowed, coarse_natural = window_order(*coarse), natural_order(*coarse)
    wider = ((0, 0), (0, few16 - few))

    def const(value):
        return jnp.asarray(value, BF16)

    operands = dict(
        tokens=tokens.reshape(cells, breadth),
        pick1=const(picker(*fine, True, natural)),
        cotangent=cotangent,
        pick_c=const(np.pad(picker(*coarse, True, coarse_natural), wider)),
        gather1=const(assembler(*fine, True, windowed, natural)),
        fine_gain=fine_gain[None],
        fine_qkv=fine_qkv,
        fine_proj=fine_proj,
        pick2=const(picker(*fine, True, windowed)),
        gather_c=const(assembler(*coarse, True, coarse_windowed, coarse_natural)),
        coarse_proj=coarse_proj,
        gather2=const(assembler(*fine, True, merged, windowed)),
        merge_gain=merge_gain[None],
        merge_weight=merge_weight,
        coarse_gain=coarse_gain[None],
        coarse_qkv=coarse_qkv,
        pick3=const(picker(*fine, False, merged)),
        pick_o=const(np.pad(picker(*coarse, False, coarse_windowed), wider)),
        gather3=const(assembler(*fine, False, windowed, merged)),
        pick4=const(picker(*fine, False, windowed)),
        gather_o=const(assembler(*coarse, False, coarse_natural, coarse_windowed)),
        gather4=const(assembler(*fine, False, natural, windowed)),
    )
    weights = dict(
        fine_qkv=fine_qkv,
        fine_proj=fine_proj,
        merge_weight=merge_weight,
        coarse_qkv=coarse_qkv,
        coarse_proj=coarse_proj,
    )
    blocks = {
        name: (value.shape[0] // devices, value.shape[1]) for name, value in weights.items()
    }
    runs = types.SimpleNamespace(**{name: shape[0] for name, shape in blocks.items()})
    wider_blocks = dict(blocks)
    wider_blocks["fine_qkv"] = (runs.fine_qkv, fine_qkv.shape[1] + 128)
    wider_blocks["coarse_proj"] = (runs.coarse_proj, depth + 256)
    outs = dict(output=((few, depth), F32), tokens=((cells, breadth), BF16))
    outs |= {name: (shape, F32) for name, shape in wider_blocks.items()}
    halo, small = sum(part_sizes(*fine, True)), sum(part_sizes(*coarse, True))
    window = WLAT * WLON
    groups = len(list(attention_groups(cells, HF, inner, 1)))
    groups2 = len(list(attention_groups(few, HC, inner2, 1)))
    share = coarse_qkv.shape[1] // 4

    def vmem(*shape, dtype=BF16):
        return pltpu.VMEM(shape, dtype)

    def slots(*shape):
        return vmem(2, 2, few16, *shape)

    bufs = dict(
        loads={name: pltpu.VMEM(value.shape, value.dtype) for name, value in operands.items()},
        cats=[vmem(cells + halo, breadth) for _ in range(4)],
        outs=[vmem(halo, breadth) for _ in range(4)],
        small_cats=[vmem(few16 + small, depth) for _ in range(2)],
        small_outs=[vmem(small, depth) for _ in range(2)],
        cot=vmem(few, depth, dtype=F32),
        unit1=vmem(cells, breadth, dtype=F32),
        rate1=vmem(cells, 1, dtype=F32),
        packed1=vmem(cells, 3 * inner, dtype=F32),
        mixed1=vmem(cells, inner, dtype=F32),
        saved1=vmem(groups, cells * HF // groups, window, dtype=F32),
        grad1=vmem(cells, 3 * inner, dtype=F32),
        mixed2=vmem(few, inner2, dtype=F32),
        saved2=vmem(groups2, few * HC // groups2, window, dtype=F32),
        grad2=vmem(few, 3 * inner2, dtype=F32),
        fq_l=vmem(2, cells, breadth // 2),
        fq_o=vmem(cells, breadth // 2),
        fq_r=vmem(2, cells, 3 * inner),
        fp_l=vmem(2, cells, inner // 2),
        fp_o=vmem(cells, inner // 2),
        fp_r=vmem(2, cells, breadth),
        cp_l=vmem(2, few16, inner2 // 2),
        cp_o=vmem(few16, inner2 // 2),
        cp_r=vmem(2, few16, depth),
        m_pieces=vmem(4, few16, breadth),
        m_l=slots(breadth),
        m_r=slots(depth),
        q_l=slots(depth),
        q_pieces=vmem(4, few16, share),
        q_r=slots(share),
        q_back=vmem(4, runs.coarse_qkv, share, dtype=F32),
        q_parts=vmem(4, runs.coarse_qkv, share, dtype=F32),
        gain1=vmem(2, 1, fine_gain.shape[0], dtype=F32),
        gain2=vmem(2, 1, merge_gain.shape[0] + coarse_gain.shape[0], dtype=F32),
    )

    def staged(block, count):
        return dict(
            first=vmem(count, lats, *block),
            land=vmem(count - 1, lats, *block),
            mid=vmem(lats, *block),
            last=vmem(lats - 1, *block),
        )

    sums = dict(
        fine_qkv=staged(wider_blocks["fine_qkv"], chips),
        fine_proj=staged(blocks["fine_proj"], chips),
        coarse_proj=staged(wider_blocks["coarse_proj"], chips),
        merge_weight=staged(blocks["merge_weight"], chips // 2),
        coarse_qkv=staged((4 * runs.coarse_qkv, share), chips // 2),
    )
    copies = 40 + 12 * lons + 8 * lats
    sems = dict(
        loads=pltpu.SemaphoreType.DMA((len(operands),)),
        sends=pltpu.SemaphoreType.DMA((copies,)),
        recvs=pltpu.SemaphoreType.DMA((copies,)),
    )
    scratch, _ = jax.tree.flatten([bufs, sums, sems])
    tree = jax.tree.structure(
        [
            {name: 0 for name in operands},
            {name: 0 for name in outs},
            jax.tree.map(lambda _: 0, bufs),
            jax.tree.map(lambda _: 0, sums),
            jax.tree.map(lambda _: 0, sems),
        ]
    )
    plan = types.SimpleNamespace(
        tree=tree,
        loads=list(operands),
        lats=lats,
        lons=lons,
        fine=fine,
        coarse=coarse,
        scale=(fine[0] * lats * fine[1] * lons // 4) ** (-0.5),
        fine_total=fine[0] * lats,
        coarse_total=coarse[0] * lats,
        runs=runs,
    )
    in_names, out_names = sorted(operands), sorted(outs)
    found = pl.pallas_call(
        functools.partial(mega_kernel, plan),
        name="swin_step",
        out_shape=[jax.ShapeDtypeStruct(*outs[name]) for name in out_names],
        in_specs=[ANY] * len(operands),
        out_specs=[VMEM] * len(outs),
        scratch_shapes=scratch,
        compiler_params=pltpu.CompilerParams(
            collective_id=0, has_side_effects=True, vmem_limit_bytes=60 * 1024 * 1024
        ),
        cost_estimate=pl.CostEstimate(flops=2 * 10**10, bytes_accessed=10**7, transcendentals=0),
    )(*[operands[name] for name in in_names])
    found = dict(zip(out_names, found))
    found = [found[name] for name in outs]
    gain_runs = [v.shape[0] // devices for v in (fine_gain, merge_gain, coarse_gain)]
    results = [
        (cotangent.shape, BF16),
        ((cells, breadth), BF16),
        ((1, gain_runs[0]), F32),
        (blocks["fine_qkv"], F32),
        (blocks["fine_proj"], F32),
        ((1, gain_runs[1]), F32),
        (blocks["merge_weight"], F32),
        ((1, gain_runs[2]), F32),
        (blocks["coarse_qkv"], F32),
        (blocks["coarse_proj"], F32),
    ]
    done = list(
        pl.pallas_call(
            functools.partial(finish_kernel, coarse, gain_runs),
            name="finish",
            out_shape=[jax.ShapeDtypeStruct(shape, dtype) for shape, dtype in results],
            in_specs=[VMEM] * len(found),
            out_specs=[VMEM] * len(results),
        )(*found)
    )
    done[1] = done[1].reshape(tokens.shape)
    for k in (2, 5, 7):
        done[k] = done[k].reshape(-1)
    return tuple(done)


def solution(mesh):
    return jax.shard_map(
        local,
        mesh=mesh,
        in_specs=(
            P(LAT, LON, None),
            P(),
            P(),
            P(),
            P(),
            P(),
            P(),
            P(),
            P(),
            P(LAT, LON, None),
        ),
        out_specs=(
            P(LAT, LON, None),
            P(LAT, LON, None),
            P((LAT, LON)),
            P((LAT, LON), None),
            P((LAT, LON), None),
            P((LAT, LON)),
            P((LAT, LON), None),
            P((LAT, LON)),
            P((LAT, LON), None),
            P((LAT, LON), None),
        ),
        check_vma=False,
    )
```

```python
import functools
import itertools
import types

import jax
import jax.numpy as jnp
import numpy as np
from jax import lax
from jax.experimental import pallas as pl
from jax.experimental.pallas import tpu as pltpu
from jax.sharding import PartitionSpec as P

HF = 4
HC = 8
WLAT = 6
WLON = 12
SLAT = 3
SLON = 6


EPSILON = 1e-05


VMEM = pl.BlockSpec(memory_space=pltpu.VMEM)
ANY = pl.BlockSpec(memory_space=pl.ANY)
LAT, LON = "lat", "lon"
F32 = jnp.float32
BF16 = jnp.bfloat16


def one_hot(sources, size):
    matrix = np.zeros((len(sources), size), np.float32)
    for row, source in enumerate(sources):
        if source >= 0:
            matrix[row, source] = 1.0
    return matrix


def window_order(rows, cols):
    return [
        (a * WLAT + i, b * WLON + j)
        for a in range(rows // WLAT)
        for b in range(cols // WLON)
        for i in range(WLAT)
        for j in range(WLON)
    ]


def merge_order(rows, cols):
    return [
        (2 * a + low, 2 * b + side)
        for side in range(2)
        for low in range(2)
        for a, b in window_order(rows // 2, cols // 2)
    ]


def natural_order(rows, cols):
    return [(i, j) for i in range(rows) for j in range(cols)]


def roll_parts(rows, cols, ahead):
    if ahead:
        lat, lon = (range(SLAT), range(SLAT, rows)), (range(SLON), range(SLON, cols))
    else:
        lat = (range(rows - SLAT, rows), range(rows - SLAT))
        lon = (range(cols - SLON, cols), range(cols - SLON))
    pick = ((lat[0], lon[1]), (lat[1], lon[0]), (lat[0], lon[0]))
    return [[(i, j) for i in r for j in c] for r, c in pick]


def roll_matrices(rows, cols, ahead, order):
    shift = 1 if ahead else -1
    parts = [{cell: k for k, cell in enumerate(p)} for p in roll_parts(rows, cols, ahead)]
    found = [[], [], [], []]
    for i, j in order:
        row, col = i + shift * SLAT, j + shift * SLON
        out_row, out_col = not 0 <= row < rows, not 0 <= col < cols
        cell = (row % rows, col % cols)
        which = {(0, 0): 0, (1, 0): 1, (0, 1): 2, (1, 1): 3}[(int(out_row), int(out_col))]
        for k in range(4):
            found[k].append((cell if k == 0 else parts[k - 1][cell]) if k == which else -1)
    return found, [len(p) for p in parts]


def assembling(rows, cols, ahead, order, stored):
    place = {cell: k for k, cell in enumerate(stored)}
    found, sizes = roll_matrices(rows, cols, ahead, order)
    own = [place[c] if c != -1 else -1 for c in found[0]]
    return [one_hot(own, rows * cols)] + [one_hot(f, n) for f, n in zip(found[1:], sizes)]


def sending(rows, cols, ahead, stored):
    place = {cell: k for k, cell in enumerate(stored)}
    return [
        one_hot([place[c] for c in part], rows * cols) for part in roll_parts(rows, cols, ahead)
    ]


def mm(left, right):
    return jnp.dot(left, right, preferred_element_type=F32)


def mm_t(left, right):
    return lax.dot_general(left, right, (((1,), (1,)), ((), ())), preferred_element_type=F32)


def t_mm(left, right):
    return lax.dot_general(left, right, (((0,), (0,)), ((), ())), preferred_element_type=F32)


def norm_parts(values):
    center = jnp.mean(values, axis=-1, keepdims=True)
    shifted = values - center
    spread = jnp.mean(shifted * shifted, axis=-1, keepdims=True)
    rate = lax.rsqrt(spread + EPSILON)
    return shifted * rate, rate


def norm_back(grad, unit, rate, gains):
    scaled = grad * gains
    first = jnp.mean(scaled, axis=-1, keepdims=True)
    second = jnp.mean(scaled * unit, axis=-1, keepdims=True)
    return rate * (scaled - first - unit * second), jnp.sum(grad * unit, axis=0, keepdims=True)


def lane_halves(value, size):
    lane = lax.broadcasted_iota(jnp.int32, value.shape, 1)
    return [
        jnp.where((lane >= k * size) & (lane < (k + 1) * size), value, jnp.zeros_like(value))
        for k in range(value.shape[1] // size)
    ]


def stacked(value, size):
    return jnp.concatenate(lane_halves(value, size), axis=0).astype(BF16)


def unstacked(value, size):
    cells = value.shape[0] * size // value.shape[1]
    lane = lax.broadcasted_iota(jnp.int32, (cells, value.shape[1]), 1)
    total = value[:cells]
    for k in range(1, value.shape[1] // size):
        total = jnp.where(lane >= k * size, value[k * cells : (k + 1) * cells], total)
    return total


def weights_of(query, keys, border, size):
    cells = keys.shape[0]
    scores = mm_t(query, keys) * size ** (-0.5)
    row = lax.broadcasted_iota(jnp.int32, scores.shape, 0)
    other = lax.broadcasted_iota(jnp.int32, scores.shape, 1)
    for _ in range(query.shape[0] // cells - 1):
        row = jnp.where(row >= cells, row - cells, row)
    allowed = (row >= border).astype(jnp.int32) == (other >= border).astype(jnp.int32)
    scores = jnp.where(allowed, scores, -1000000000.0)
    exponent = jnp.exp(scores - jnp.max(scores, axis=-1, keepdims=True))
    return exponent * (1.0 / jnp.sum(exponent, axis=-1, keepdims=True)), allowed


def attention_groups(cells, heads, inner, windows_lon):
    size = inner // heads
    lanes = 128 if inner % 128 == 0 and 128 % size == 0 else inner
    count = WLAT * WLON
    for window in range(cells // count):
        for start in range(0, inner, lanes):
            rows = slice(window * count, (window + 1) * count)
            yield window // windows_lon, rows, start, lanes, size


def border_of(edge, window_row):
    return (edge - window_row * WLAT) * WLON


def rounded(value):
    return value.astype(BF16).astype(F32)


def attend(packed, mixed_ref, saved, edge, heads, windows_lon):
    inner = packed.shape[1] // 3
    for k, (w, rows, start, lanes, size) in enumerate(
        attention_groups(packed.shape[0], heads, inner, windows_lon)
    ):
        query = stacked(packed[rows, start : start + lanes], size)
        keys = packed[rows, inner + start : inner + start + lanes].astype(BF16)
        vals = packed[rows, 2 * inner + start : 2 * inner + start + lanes].astype(BF16)
        weights, _ = weights_of(query, keys, border_of(edge, w), size)
        saved[k] = weights
        mixed_ref[rows, start : start + lanes] = unstacked(mm(weights.astype(BF16), vals), size)


def attend_back(packed, grad_mixed, grad_ref, saved, edge, heads, windows_lon, between=None):
    inner = packed.shape[1] // 3
    for k, (w, rows, start, lanes, size) in enumerate(
        attention_groups(packed.shape[0], heads, inner, windows_lon)
    ):
        query = stacked(packed[rows, start : start + lanes], size)
        keys = packed[rows, inner + start : inner + start + lanes].astype(BF16)
        vals = packed[rows, 2 * inner + start : 2 * inner + start + lanes].astype(BF16)
        grad = stacked(grad_mixed[rows, start : start + lanes], size)
        weights = saved[k]
        allowed = allowed_of(weights.shape, WLAT * WLON, border_of(edge, w))
        grad_weights = mm_t(grad, vals).astype(BF16).astype(F32)
        grad_vals = t_mm(weights.astype(BF16), grad)
        along = jnp.sum(grad_weights * weights, axis=-1, keepdims=True)
        slope = jnp.where(allowed, weights * (grad_weights - along), 0.0) * size ** (-0.5)
        slope = slope.astype(BF16)
        grad_ref[rows, start : start + lanes] = unstacked(mm(slope, keys), size)
        grad_ref[rows, inner + start : inner + start + lanes] = t_mm(slope, query)
        grad_ref[rows, 2 * inner + start : 2 * inner + start + lanes] = grad_vals
        if between is not None:
            between(k)


def allowed_of(shape, cells, border):
    row = lax.broadcasted_iota(jnp.int32, shape, 0)
    other = lax.broadcasted_iota(jnp.int32, shape, 1)
    for _ in range(shape[0] // cells - 1):
        row = jnp.where(row >= cells, row - cells, row)
    return (row >= border).astype(jnp.int32) == (other >= border).astype(jnp.int32)


def up16(count):
    return -(-count // 16) * 16


def part_sizes(rows, cols, ahead):
    return [up16(len(part)) for part in roll_parts(rows, cols, ahead)]


def assembler(rows, cols, ahead, order, stored):
    pieces = []
    for matrix in assembling(rows, cols, ahead, order, stored):
        width = matrix.shape[1]
        pieces.append(np.pad(np.asarray(matrix, np.float32), ((0, 0), (0, up16(width) - width))))
    return np.concatenate(pieces, axis=1)


def picker(rows, cols, ahead, stored):
    pieces = []
    for matrix in sending(rows, cols, ahead, stored):
        height = matrix.shape[0]
        pieces.append(np.pad(np.asarray(matrix, np.float32), ((0, up16(height) - height), (0, 0))))
    return np.concatenate(pieces, axis=0)


def padded(value):
    extra = up16(value.shape[0]) - value.shape[0]
    if extra:
        value = jnp.concatenate([value, jnp.zeros((extra, value.shape[1]), value.dtype)], axis=0)
    return value


def parity_matrix(run, parity):
    shape = (256, 256)
    source = lax.broadcasted_iota(jnp.int32, shape, 0)
    target = lax.broadcasted_iota(jnp.int32, shape, 1)
    side = (target // 128 + parity) % 2
    wanted = ((target % 128) // run * 2 + side) * run + target % run
    return (source == wanted).astype(F32).astype(BF16)


def by_parity(value, matrix):
    parts = [mm(value[:, b : b + 256], matrix) for b in range(0, value.shape[1], 256)]
    mine = jnp.concatenate([part[:, :128] for part in parts], axis=1).astype(BF16)
    other = jnp.concatenate([part[:, 128:] for part in parts], axis=1).astype(BF16)
    return mine, other


def joined(ref):
    value = ref[...]
    return value.reshape(value.shape[0] * value.shape[1], value.shape[2])


class Links:
    def __init__(self, lats, lons, sends, recvs):
        self.lats, self.lons, self.sends, self.recvs = lats, lons, sends, recvs
        self.lat, self.lon = lax.axis_index(LAT), lax.axis_index(LON)
        self.side, self.chip, self.chips = self.lon % 2, self.lon // 2, lons // 2
        self.ids, self.started = itertools.count(), []

    def at(self, lat_step, lon_step):
        lat = (self.lat + lat_step + self.lats) % self.lats
        return (lat, (self.lon + lon_step + self.lons) % self.lons)

    def partner(self):
        return (self.lat, self.lon + 1 - 2 * self.side)

    def chip_of(self, ahead):
        return (self.chip + ahead) % self.chips

    def same_side(self, ahead):
        return (self.lat, 2 * self.chip_of(ahead) + self.side)

    def send(self, source, target, device):
        index = next(self.ids)
        copy = pltpu.make_async_remote_copy(
            src_ref=source,
            dst_ref=target,
            send_sem=self.sends.at[index],
            recv_sem=self.recvs.at[index],
            device_id=device,
            device_id_type=pl.DeviceIdType.MESH,
        )
        copy.start()
        self.started.append(copy)
        return copy

    def greet(self):
        peers = [self.at(a, b) for s in (-1, 1) for a, b in ((s, 0), (0, s), (s, s))]
        peers += [self.at(0, step) for step in range(1, self.lons)]
        peers += [self.at(step, 0) for step in range(1, self.lats)]
        barrier = pltpu.get_barrier_semaphore()
        for peer in peers:
            pl.semaphore_signal(
                barrier, inc=1, device_id=peer, device_id_type=pl.DeviceIdType.MESH
            )
        return lambda: pl.semaphore_wait(barrier, len(peers))

    def exchange(self, out, target, own, sizes, ahead):
        s = -1 if ahead else 1
        copies, begin = [], 0
        for size, (a, b) in zip(sizes, ((s, 0), (0, s), (s, s))):
            there = target.at[pl.ds(own + begin, size)]
            copies.append(self.send(out.at[pl.ds(begin, size)], there, self.at(a, b)))
            begin += size
        return copies

    def near(self, level):
        step = 1 << level
        bit = (self.chip // step) % 2
        rest = self.chip // (2 * step) * step + self.chip % step
        count = self.chips // 2

        def at_rest(ahead):
            place = (rest + ahead) % count
            chip = place // step * (2 * step) + bit * step + place % step
            return (self.lat, 2 * chip + self.side)

        chip = self.chip + step - 2 * step * bit
        found = types.SimpleNamespace(bit=bit, quarter=2 * bit + self.side)
        found.same = (self.lat, 2 * chip + self.side)
        found.other = (self.lat, 2 * chip + 1 - self.side)
        found.ring = types.SimpleNamespace(place=rest, count=count, device=at_rest)
        return found

    def flipped(self):
        return (self.lat + 1 - 2 * (self.lat % 2), self.lon)

    def column(self):
        return types.SimpleNamespace(
            place=self.lat, count=self.lats, device=lambda ahead: self.at(ahead, 0)
        )

    def plane(self):
        return types.SimpleNamespace(place=self.chip, count=self.chips, device=self.same_side)

    def spread(self, slots, near):
        return [
            self.send(slots.at[0, 0], slots.at[1, 0], self.partner()),
            self.send(slots.at[0, 0], slots.at[0, 1], near.same),
        ]

    def relay(self, slots, copies):
        arrive(copies[1:])
        return copies[:1] + [self.send(slots.at[0, 1], slots.at[1, 1], self.partner())]

    def deal(self, pieces, slots, near):
        slots[0, 0] = pieces[near.quarter]
        mine, flip = 2 * near.bit, 2 - 2 * near.bit
        return [
            self.send(pieces.at[flip + self.side], slots.at[0, 1], near.same),
            self.send(pieces.at[flip + 1 - self.side], slots.at[1, 1], near.other),
            self.send(pieces.at[mine + 1 - self.side], slots.at[1, 0], self.partner()),
        ]


def arrive(copies):
    for copy in copies:
        copy.wait_recv()


class Sums:
    def __init__(self, links, ring, second, bufs, out, scale):
        self.links, self.ring, self.second, self.bufs = links, ring, second, bufs
        self.halved = hasattr(bufs, "half")
        self.out, self.scale = out, scale

    def begin(self):
        links, ring, bufs = self.links, self.ring, self.bufs
        self.copies = []
        for ahead in range(1, ring.count):
            source = bufs.first.at[(ring.place + ahead) % ring.count]
            self.copies.append(links.send(source, bufs.land.at[ahead - 1], ring.device(ahead)))

    def middle(self):
        ring, bufs = self.ring, self.bufs
        arrive(self.copies)
        for k in range(self.second.count):
            total = bufs.first[ring.place, k].astype(F32)
            for ahead in range(1, ring.count):
                total = total + bufs.land[ahead - 1, k].astype(F32)
            place = k % 2 * (self.second.count // 2) + k // 2 if self.halved else k
            bufs.mid[place] = total.astype(bufs.mid.dtype)
        self.across()

    def across(self):
        links, ring, bufs = self.links, self.second, self.bufs
        self.copies = []
        if self.halved:
            count = ring.count // 2
            source = bufs.mid.at[pl.ds((1 - ring.place % 2) * count, count)]
            self.copies.append(links.send(source, bufs.half, links.flipped()))
            return
        for ahead in range(1, ring.count):
            source = bufs.mid.at[(ring.place + ahead) % ring.count]
            self.copies.append(links.send(source, bufs.last.at[ahead - 1], ring.device(ahead)))

    def halve(self):
        links, ring, bufs = self.links, self.second, self.bufs
        arrive(self.copies)
        count = ring.count // 2
        for k in range(count):
            total = bufs.mid[ring.place % 2 * count + k].astype(F32) + bufs.half[k].astype(F32)
            bufs.high[k] = total.astype(bufs.high.dtype)
        self.copies = []
        for ahead in range(1, count):
            source = bufs.high.at[(ring.place // 2 + ahead) % count]
            there = ring.device(2 * ahead)
            self.copies.append(links.send(source, bufs.last.at[ahead - 1], there))

    def end(self):
        ring, bufs = self.second, self.bufs
        arrive(self.copies)
        own = bufs.high[ring.place // 2] if self.halved else bufs.mid[ring.place]
        total = own.astype(F32)
        for ahead in range(1, ring.count // 2 if self.halved else ring.count):
            total = total + bufs.last[ahead - 1].astype(F32)
        self.total = total * self.scale
        if self.out is not None:
            self.out[...] = self.total


def flat(ref):
    value = ref[...]
    count = 1
    for size in value.shape[:-1]:
        count *= size
    return value.reshape(count, value.shape[-1])


def mega_kernel(plan, *refs):
    tree = jax.tree.unflatten(plan.tree, refs)
    ins, res, buf, sums, sems = [types.SimpleNamespace(**part) for part in tree]
    lats, lons, fine, coarse, runs = plan.lats, plan.lons, plan.fine, plan.coarse, plan.runs
    links = Links(lats, lons, sems.sends, sems.recvs)
    cells, few = fine[0] * fine[1], coarse[0] * coarse[1]
    few16 = up16(few)
    wide, fine_wide = coarse[1] // WLON, fine[1] // WLON
    chips = lons // 2
    greeted = links.greet()

    loads = {}
    for k, name in enumerate(plan.loads):
        loads[name] = pltpu.make_async_copy(getattr(ins, name), buf.loads[name], sems.loads.at[k])
        loads[name].start()

    def load(name):
        if name in loads:
            loads.pop(name).wait()
        return buf.loads[name][...]

    names = types.SimpleNamespace(**{name: name for name in plan.loads})
    sizes, back_sizes = part_sizes(*fine, True), part_sizes(*fine, False)
    small, small_back = part_sizes(*coarse, True), part_sizes(*coarse, False)
    cat1, cat2, cat3, cat4 = buf.cats
    out1, out2, out3, out4 = buf.outs
    cat_c, cat_o = buf.small_cats
    out_c, out_o = buf.small_outs

    own_tokens = load(names.tokens)
    cat1[0:cells] = own_tokens
    out1[...] = mm(load(names.pick1), own_tokens).astype(BF16)
    greeted()
    halo1 = links.exchange(out1, cat1, cells, sizes, True)
    grid = load(names.cotangent)
    for i in range(coarse[0]):
        buf.cot[i * coarse[1] : (i + 1) * coarse[1]] = grid[i].astype(F32)
    own_cot = padded(buf.cot[...]).astype(BF16)
    cat_c[0:few16] = own_cot
    out_c[...] = mm(load(names.pick_c), own_cot).astype(BF16)
    halo_c = links.exchange(out_c, cat_c, few16, small, True)
    edge = plan.fine_total - SLAT - links.lat * fine[0]
    coarse_edge = plan.coarse_total - SLAT - links.lat * coarse[0]
    split = {
        run: parity_matrix(run, links.side)
        for run in sorted({runs.fine_qkv, runs.fine_proj, runs.coarse_proj})
    }

    gather1 = load(names.gather1)
    arrive(halo1)
    x1 = mm(gather1, cat1[...])
    unit1, rate1 = norm_parts(x1)
    gains1 = load(names.fine_gain)
    normed1 = (unit1 * gains1).astype(BF16)
    buf.unit1[...] = unit1
    buf.rate1[...] = rate1
    w_qkv1 = load(names.fine_qkv)
    packed1 = rounded(mm(normed1, w_qkv1))
    buf.packed1[...] = packed1
    attend(packed1, buf.mixed1, buf.saved1, edge, HF, fine_wide)
    blend1 = buf.mixed1[...].astype(BF16)
    w_proj1 = load(names.fine_proj)
    y1 = (x1 + mm(blend1, w_proj1)).astype(BF16)
    cat2[0:cells] = y1
    out2[...] = mm(load(names.pick2), y1).astype(BF16)
    halo2 = links.exchange(out2, cat2, cells, sizes, True)

    def to_partner(pair):
        return links.send(pair.at[0], pair.at[1], links.partner())

    def halves(value, run, pair, out):
        mine, other = by_parity(value, split[run])
        pair[0] = mine
        out[...] = other
        return links.send(out, pair.at[1], links.partner())

    pair_fq = halves(normed1, runs.fine_qkv, buf.fq_l, buf.fq_o)
    pair_fp = halves(blend1, runs.fine_proj, buf.fp_l, buf.fp_o)
    gather_c = load(names.gather_c)
    arrive(halo_c)
    dy2 = mm(gather_c, cat_c[...])
    buf.cp_r[0] = padded(dy2).astype(BF16)
    pair_dy2 = to_partner(buf.cp_r)
    w_proj2 = load(names.coarse_proj)
    grad_mixed2 = rounded(mm_t(dy2.astype(BF16), w_proj2))
    gather2 = load(names.gather2)
    merge_gains, w_merge = load(names.merge_gain), load(names.merge_weight)
    gains2, w_qkv2 = load(names.coarse_gain), load(names.coarse_qkv)
    arrive(halo2)

    spread = mm(gather2, cat2[...])
    packed_grid = jnp.concatenate([spread[k * few : (k + 1) * few] for k in range(4)], axis=1)
    merge_unit, merge_rate = norm_parts(packed_grid)
    merge_scaled = padded(merge_unit * merge_gains)
    merge_normed = merge_scaled.astype(BF16)
    x2 = rounded(mm(merge_normed, w_merge)[:few])
    near_m, near_q = links.near(min(1, chips.bit_length() - 2)), links.near(0)
    run = runs.merge_weight
    level = min(1, chips.bit_length() - 2)
    for q in range(4):
        parts = []
        for r in range(chips // 2):
            chip = (r >> level << level + 1) + (q // 2 << level) + r % (1 << level)
            parts += [((k * chips + chip) * 2 + q % 2) * run for k in range(lats)]
        piece = jnp.concatenate([merge_scaled[:, p : p + run] for p in parts], axis=1)
        buf.m_pieces[q] = piece.astype(BF16)
    sent_m = links.deal(buf.m_pieces, buf.m_l, near_m)
    unit2, rate2 = norm_parts(x2)
    normed2 = padded(unit2 * gains2).astype(BF16)
    buf.q_l[0, 0] = normed2
    sent_n = links.spread(buf.q_l, near_q)
    packed2 = rounded(mm(normed2, w_qkv2)[:few])
    attend(packed2, buf.mixed2, buf.saved2, coarse_edge, HC, wide)
    blend2 = padded(buf.mixed2[...]).astype(BF16)
    pair_p = halves(blend2, runs.coarse_proj, buf.cp_l, buf.cp_o)

    def sum_of(name, out, ring, second=None):
        bufs = types.SimpleNamespace(**getattr(sums, name))
        return Sums(links, ring, second or links.column(), bufs, out, plan.scale)

    keys = types.SimpleNamespace(**{name: name for name in vars(sums)})
    total_p = sum_of(keys.coarse_proj, res.coarse_proj, links.column(), links.plane())
    total_q = sum_of(keys.coarse_qkv, None, near_q.ring)
    total_m = sum_of(keys.merge_weight, res.merge_weight, near_m.ring)
    total_fp = sum_of(keys.fine_proj, res.fine_proj, links.plane())
    total_fq = sum_of(keys.fine_qkv, res.fine_qkv, links.plane())

    def reduced(left, right, run, total, by_row=False):
        value = t_mm(flat(left), flat(right))
        width = value.shape[1]
        for row in range(lats):
            for chip in range(chips):
                begin = (row * chips + chip) * run
                piece = value[begin : begin + run].astype(BF16)
                place = (row, chip) if by_row else (chip, row)
                total.bufs.first[place[0], place[1], :, 0:width] = piece
        return width

    def between2(k):
        if k == 1:
            arrive([pair_p, pair_dy2])
            reduced(buf.cp_l, buf.cp_r, runs.coarse_proj, total_p, True)
            total_p.begin()

    attend_back(
        packed2, grad_mixed2, buf.grad2, buf.saved2, coarse_edge, HC, wide, between2
    )
    grad2 = padded(buf.grad2[...])
    grad_packed2 = grad2.astype(BF16)
    share = grad2.shape[1] // 4
    for q in range(4):
        buf.q_pieces[q] = grad2[:, q * share : (q + 1) * share].astype(BF16)
    sent_q = links.deal(buf.q_pieces, buf.q_r, near_q)

    place = lax.broadcasted_iota(jnp.int32, (lats * chips, 128), 0)
    lane = lax.broadcasted_iota(jnp.int32, (lats * chips, 128), 1)
    owner = (place % lats) * lons + (place // lats) * 2 + links.side
    fold_row = lax.broadcasted_iota(jnp.int32, (128, 128), 0)
    fold_col = lax.broadcasted_iota(jnp.int32, (128, 128), 1)

    def deal_gains(value, total, start):
        run = value.shape[1] // (lats * lons)
        picked = jnp.zeros((lats * chips, 128), F32)
        for b in range(0, value.shape[1], 128):
            row = jnp.broadcast_to(value[:, b : b + 128], (lats * chips, 128))
            picked = picked + jnp.where((lane + b) // run == owner, row, 0.0)
        fold = (fold_row % run == fold_col).astype(BF16)
        folded = mm(picked.astype(BF16), fold)
        target = total.bufs.first
        shape = (target.shape[2], 128)
        for p in range(lats * chips):
            rows = jnp.broadcast_to(folded[p : p + 1], shape).astype(BF16)
            target[p // lats, p % lats, :, start : start + 128] = rows

    grad_normed2 = rounded(mm_t(grad_packed2, w_qkv2)[:few])
    grad_in2, gain_sum2 = norm_back(grad_normed2, unit2, rate2, gains2)
    dz = padded(dy2 + grad_in2).astype(BF16)
    buf.m_r[0, 0] = dz
    sent_z = links.spread(buf.m_r, near_m)
    grad_merge = rounded(mm_t(dz, w_merge)[:few])
    grad_grid, merge_sum = norm_back(grad_merge, merge_unit, merge_rate, merge_gains)
    breadth = spread.shape[1]
    df = jnp.concatenate(
        [grad_grid[:, k * breadth : (k + 1) * breadth] for k in range(4)], axis=0
    ).astype(BF16)
    cat3[0:cells] = df
    out3[...] = mm(load(names.pick3), df).astype(BF16)
    halo3 = links.exchange(out3, cat3, cells, back_sizes, False)
    merge_count = merge_sum.shape[1]
    buf.gain2[0, :, 0:merge_count] = merge_sum
    buf.gain2[0, :, merge_count:] = gain_sum2
    pair_g2 = to_partner(buf.gain2)
    relay_n = links.relay(buf.q_l, sent_n)

    result2 = padded(x2 + mm(blend2, w_proj2)[:few]).astype(BF16)
    cat_o[0:few16] = result2
    out_o[...] = mm(load(names.pick_o), result2).astype(BF16)
    halo_o = links.exchange(out_o, cat_o, few16, small_back, False)
    relay_z = links.relay(buf.m_r, sent_z)
    steps = types.SimpleNamespace()

    def reduce_near(left, right, total, by_row):
        value = t_mm(flat(left), flat(right))
        count = total.ring.count
        tall = value.shape[0] // (lats * count)
        for row in range(lats):
            for place in range(count):
                begin = (row * count + place if by_row else place * lats + row) * tall
                total.bufs.first[place, row] = value[begin : begin + tall].astype(BF16)
        total.begin()

    arrive(sent_q + relay_n)
    reduce_near(buf.q_l, buf.q_r, total_q, True)
    arrive(relay_z + sent_m)
    reduce_near(buf.m_l, buf.m_r, total_m, False)
    gather3 = load(names.gather3)
    arrive(halo3)

    dy1 = mm(gather3, cat3[...])
    dy1_low = dy1.astype(BF16)
    buf.fp_r[0] = dy1_low
    pair_dy1 = to_partner(buf.fp_r)
    grad_mixed1 = rounded(mm_t(dy1_low, w_proj1))

    def between1(k):
        if k == 2:
            arrive([pair_fp, pair_dy1, pair_g2])
            width_p = reduced(buf.fp_l, buf.fp_r, runs.fine_proj, total_fp)
            gains_both = buf.gain2[0] + buf.gain2[1]
            deal_gains(gains_both[:, :merge_count], total_fp, width_p)
            deal_gains(gains_both[:, merge_count:], total_fp, width_p + 128)
            total_fp.begin()
        if k == 0:
            total_p.middle()
        if k == 7:
            total_q.middle()

    attend_back(
        buf.packed1[...], grad_mixed1, buf.grad1, buf.saved1, edge, HF, fine_wide, between1
    )
    grad_packed1 = buf.grad1[...].astype(BF16)
    buf.fq_r[0] = grad_packed1
    pair_dp1 = to_partner(buf.fq_r)
    grad_normed1 = rounded(mm_t(grad_packed1, w_qkv1))
    grad_in1, gain_sum1 = norm_back(grad_normed1, buf.unit1[...], buf.rate1[...], gains1)
    buf.gain1[0] = gain_sum1
    pair_g1 = to_partner(buf.gain1)
    dx1 = (dy1 + grad_in1).astype(BF16)
    cat4[0:cells] = dx1
    out4[...] = mm(load(names.pick4), dx1).astype(BF16)
    halo4 = links.exchange(out4, cat4, cells, back_sizes, False)
    arrive([pair_fq, pair_dp1])
    width_q = reduced(buf.fq_l, buf.fq_r, runs.fine_qkv, total_fq)
    arrive([pair_g1])
    deal_gains(buf.gain1[0] + buf.gain1[1], total_fq, width_q)
    total_fq.begin()
    total_q.halve()
    total_m.middle()
    total_p.end()
    total_fp.middle()
    total_q.end()
    for q in range(4):
        high = total_q.total.shape[0] // 4
        buf.q_back[q] = total_q.total[q * high : (q + 1) * high]
    buf.q_parts[near_q.quarter] = buf.q_back[near_q.quarter]
    target = buf.q_parts.at[near_q.quarter]
    mine, flip = 2 * near_q.bit, 2 - 2 * near_q.bit
    sent_back = [
        links.send(buf.q_back.at[flip + links.side], target, near_q.same),
        links.send(buf.q_back.at[flip + 1 - links.side], target, near_q.other),
        links.send(buf.q_back.at[mine + 1 - links.side], target, links.partner()),
    ]
    arrive(halo_o)
    res.output[...] = mm(load(names.gather_o), cat_o[...])
    total_m.halve()
    gather4 = load(names.gather4)
    arrive(halo4)
    res.tokens[...] = mm(gather4, cat4[...]).astype(BF16)
    total_fq.middle()
    arrive(sent_back)
    for q in range(4):
        res.coarse_qkv[:, q * share : (q + 1) * share] = buf.q_parts[q]
    total_fp.end()
    total_m.end()
    total_fq.end()
    for copy in links.started:
        copy.wait_send()


def finish_kernel(coarse, runs, *refs):
    ins, outs = refs[:7], refs[7:]
    output, tokens, qkv1, proj1, merge, qkv2, proj2 = ins
    for i in range(coarse[0]):
        outs[0][i] = output[i * coarse[1] : (i + 1) * coarse[1]].astype(BF16)
    outs[1][...] = tokens[...]
    for k, value in ((3, qkv1), (4, proj1), (6, merge), (8, qkv2), (9, proj2)):
        outs[k][...] = value[:, : outs[k].shape[1]]
    wide1, wide2 = outs[3].shape[1], outs[4].shape[1]
    for k, value, begin in ((2, qkv1, wide1), (5, proj1, wide2), (7, proj1, wide2 + 128)):
        outs[k][...] = value[0:1, begin : begin + outs[k].shape[1]]


def local(
    tokens,
    fine_gain,
    fine_qkv,
    fine_proj,
    merge_gain,
    merge_weight,
    coarse_gain,
    coarse_qkv,
    coarse_proj,
    cotangent,
):
    lats, lons = lax.axis_size(LAT), lax.axis_size(LON)
    devices, chips = lats * lons, lons // 2
    fine = tokens.shape[:2]
    coarse = (fine[0] // 2, fine[1] // 2)
    cells, few = fine[0] * fine[1], coarse[0] * coarse[1]
    few16 = up16(few)
    breadth, inner, inner2 = tokens.shape[2], fine_proj.shape[0], coarse_proj.shape[0]
    depth = coarse_proj.shape[1]
    windowed, natural, merged = window_order(*fine), natural_order(*fine), merge_order(*fine)
    coarse_windowed, coarse_natural = window_order(*coarse), natural_order(*coarse)
    wider = ((0, 0), (0, few16 - few))

    def const(value):
        return jnp.asarray(value, BF16)

    operands = dict(
        tokens=tokens.reshape(cells, breadth),
        pick1=const(picker(*fine, True, natural)),
        cotangent=cotangent,
        pick_c=const(np.pad(picker(*coarse, True, coarse_natural), wider)),
        gather1=const(assembler(*fine, True, windowed, natural)),
        fine_gain=fine_gain[None],
        fine_qkv=fine_qkv,
        fine_proj=fine_proj,
        pick2=const(picker(*fine, True, windowed)),
        gather_c=const(assembler(*coarse, True, coarse_windowed, coarse_natural)),
        coarse_proj=coarse_proj,
        gather2=const(assembler(*fine, True, merged, windowed)),
        merge_gain=merge_gain[None],
        merge_weight=merge_weight,
        coarse_gain=coarse_gain[None],
        coarse_qkv=coarse_qkv,
        pick3=const(picker(*fine, False, merged)),
        pick_o=const(np.pad(picker(*coarse, False, coarse_windowed), wider)),
        gather3=const(assembler(*fine, False, windowed, merged)),
        pick4=const(picker(*fine, False, windowed)),
        gather_o=const(assembler(*coarse, False, coarse_natural, coarse_windowed)),
        gather4=const(assembler(*fine, False, natural, windowed)),
    )
    weights = dict(
        fine_qkv=fine_qkv,
        fine_proj=fine_proj,
        merge_weight=merge_weight,
        coarse_qkv=coarse_qkv,
        coarse_proj=coarse_proj,
    )
    blocks = {
        name: (value.shape[0] // devices, value.shape[1]) for name, value in weights.items()
    }
    runs = types.SimpleNamespace(**{name: shape[0] for name, shape in blocks.items()})
    wider_blocks = dict(blocks)
    wider_blocks["fine_qkv"] = (runs.fine_qkv, fine_qkv.shape[1] + 128)
    wider_blocks["fine_proj"] = (runs.fine_proj, breadth + 256)
    outs = dict(output=((few, depth), F32), tokens=((cells, breadth), BF16))
    outs |= {name: (shape, F32) for name, shape in wider_blocks.items()}
    halo, small = sum(part_sizes(*fine, True)), sum(part_sizes(*coarse, True))
    window = WLAT * WLON
    groups = len(list(attention_groups(cells, HF, inner, 1)))
    groups2 = len(list(attention_groups(few, HC, inner2, 1)))
    share = coarse_qkv.shape[1] // 4

    def vmem(*shape, dtype=BF16):
        return pltpu.VMEM(shape, dtype)

    def slots(*shape):
        return vmem(2, 2, few16, *shape)

    bufs = dict(
        loads={name: pltpu.VMEM(value.shape, value.dtype) for name, value in operands.items()},
        cats=[vmem(cells + halo, breadth) for _ in range(4)],
        outs=[vmem(halo, breadth) for _ in range(4)],
        small_cats=[vmem(few16 + small, depth) for _ in range(2)],
        small_outs=[vmem(small, depth) for _ in range(2)],
        cot=vmem(few, depth, dtype=F32),
        unit1=vmem(cells, breadth, dtype=F32),
        rate1=vmem(cells, 1, dtype=F32),
        packed1=vmem(cells, 3 * inner, dtype=F32),
        mixed1=vmem(cells, inner, dtype=F32),
        saved1=vmem(groups, cells * HF // groups, window, dtype=F32),
        grad1=vmem(cells, 3 * inner, dtype=F32),
        mixed2=vmem(few, inner2, dtype=F32),
        saved2=vmem(groups2, few * HC // groups2, window, dtype=F32),
        grad2=vmem(few, 3 * inner2, dtype=F32),
        fq_l=vmem(2, cells, breadth // 2),
        fq_o=vmem(cells, breadth // 2),
        fq_r=vmem(2, cells, 3 * inner),
        fp_l=vmem(2, cells, inner // 2),
        fp_o=vmem(cells, inner // 2),
        fp_r=vmem(2, cells, breadth),
        cp_l=vmem(2, few16, inner2 // 2),
        cp_o=vmem(few16, inner2 // 2),
        cp_r=vmem(2, few16, depth),
        m_pieces=vmem(4, few16, breadth),
        m_l=slots(breadth),
        m_r=slots(depth),
        q_l=slots(depth),
        q_pieces=vmem(4, few16, share),
        q_r=slots(share),
        q_back=vmem(4, runs.coarse_qkv, share, dtype=F32),
        q_parts=vmem(4, runs.coarse_qkv, share, dtype=F32),
        gain1=vmem(2, 1, fine_gain.shape[0], dtype=F32),
        gain2=vmem(2, 1, merge_gain.shape[0] + coarse_gain.shape[0], dtype=F32),
    )

    def staged(block, count, second=lats, halved=False):
        found = dict(
            first=vmem(count, second, *block),
            land=vmem(count - 1, second, *block),
            mid=vmem(second, *block),
            last=vmem(second // 2 - 1 if halved else second - 1, *block),
        )
        if halved:
            found |= dict(half=vmem(second // 2, *block), high=vmem(second // 2, *block))
        return found

    sums = dict(
        fine_qkv=staged(wider_blocks["fine_qkv"], chips),
        fine_proj=staged(wider_blocks["fine_proj"], chips),
        coarse_proj=staged(blocks["coarse_proj"], lats, chips),
        merge_weight=staged(blocks["merge_weight"], chips // 2, halved=True),
        coarse_qkv=staged((4 * runs.coarse_qkv, share), chips // 2, halved=True),
    )
    copies = 40 + 12 * lons + 8 * lats
    sems = dict(
        loads=pltpu.SemaphoreType.DMA((len(operands),)),
        sends=pltpu.SemaphoreType.DMA((copies,)),
        recvs=pltpu.SemaphoreType.DMA((copies,)),
    )
    scratch, _ = jax.tree.flatten([bufs, sums, sems])
    tree = jax.tree.structure(
        [
            {name: 0 for name in operands},
            {name: 0 for name in outs},
            jax.tree.map(lambda _: 0, bufs),
            jax.tree.map(lambda _: 0, sums),
            jax.tree.map(lambda _: 0, sems),
        ]
    )
    plan = types.SimpleNamespace(
        tree=tree,
        loads=list(operands),
        lats=lats,
        lons=lons,
        fine=fine,
        coarse=coarse,
        scale=(fine[0] * lats * fine[1] * lons // 4) ** (-0.5),
        fine_total=fine[0] * lats,
        coarse_total=coarse[0] * lats,
        runs=runs,
    )
    in_names, out_names = sorted(operands), sorted(outs)
    found = pl.pallas_call(
        functools.partial(mega_kernel, plan),
        name="swin_step",
        out_shape=[jax.ShapeDtypeStruct(*outs[name]) for name in out_names],
        in_specs=[ANY] * len(operands),
        out_specs=[VMEM] * len(outs),
        scratch_shapes=scratch,
        compiler_params=pltpu.CompilerParams(
            collective_id=0, has_side_effects=True, vmem_limit_bytes=60 * 1024 * 1024
        ),
        cost_estimate=pl.CostEstimate(flops=2 * 10**10, bytes_accessed=10**7, transcendentals=0),
    )(*[operands[name] for name in in_names])
    found = dict(zip(out_names, found))
    found = [found[name] for name in outs]
    gain_runs = [v.shape[0] // devices for v in (fine_gain, merge_gain, coarse_gain)]
    results = [
        (cotangent.shape, BF16),
        ((cells, breadth), BF16),
        ((1, gain_runs[0]), F32),
        (blocks["fine_qkv"], F32),
        (blocks["fine_proj"], F32),
        ((1, gain_runs[1]), F32),
        (blocks["merge_weight"], F32),
        ((1, gain_runs[2]), F32),
        (blocks["coarse_qkv"], F32),
        (blocks["coarse_proj"], F32),
    ]
    done = list(
        pl.pallas_call(
            functools.partial(finish_kernel, coarse, gain_runs),
            name="finish",
            out_shape=[jax.ShapeDtypeStruct(shape, dtype) for shape, dtype in results],
            in_specs=[VMEM] * len(found),
            out_specs=[VMEM] * len(results),
        )(*found)
    )
    done[1] = done[1].reshape(tokens.shape)
    for k in (2, 5, 7):
        done[k] = done[k].reshape(-1)
    return tuple(done)


def solution(mesh):
    return jax.shard_map(
        local,
        mesh=mesh,
        in_specs=(
            P(LAT, LON, None),
            P(),
            P(),
            P(),
            P(),
            P(),
            P(),
            P(),
            P(),
            P(LAT, LON, None),
        ),
        out_specs=(
            P(LAT, LON, None),
            P(LAT, LON, None),
            P((LAT, LON)),
            P((LAT, LON), None),
            P((LAT, LON), None),
            P((LAT, LON)),
            P((LAT, LON), None),
            P((LAT, LON)),
            P((LAT, LON), None),
            P((LAT, LON), None),
        ),
        check_vma=False,
    )
```
